32 devices in a mesh: row: 4 (over y, core), col: 8 (over z, x).
Axes of the slice: x: 2, y: 2, z: 4, core: 2. Of those that a mesh axis runs over, the one named last changes fastest.
Arguments:
- transition: bfloat16 [6144, 6144], P('row', 'col'), may hold values from 0 to 51.031036, as said below
- tile_pattern: int32 [48, 48], P('row', 'col'), may hold values from 0 to 1, as said below
- kept_tiles: int32 [48, 24], P('row', 'col'), may hold values from 0 to 1, as said below
Outputs:
- next_panel: float32 [6144, 3072], P('row', 'col')
- chaos: float32 [], replicated
The draws below stay inside these ranges and needn't reach their ends.
Inputs may be any that keep to these rules, and one draw needn't show every extreme that they name: `tile_pattern`: each device's block of 12 x 6 tiles holds at most 36 nonzero tiles, and some block holds exactly 36. Every diagonal tile is nonzero. `kept_tiles`: for panel tile column p, the tile in tile row (p // 3) * 6 + p % 3 is always kept. `transition`: all entries are positive.
All inputs are finite; a program needn't handle non-finite values.
Results may differ from the reference program's by a relative error of at most 0.0003.
Values may be sent and summed in bfloat16 or wider, within the bound.
No kernel may reach another device: no remote copies, remote signals or barrier semaphores. Data moves between devices by JAX's collectives and lax.ppermute only.
A program may use at most 128 MiB of HBM per device.

```python
import math
import jax
import jax.numpy as jnp

TILE = 128
RT = 12
PT = 3
NT = 48
KT = 6
KDEV = 36
NODES = 6144
PANEL = 3072
N_COL = 8


def draw_transition(key, part):
    key_base, key_rows, key_cols = jax.random.split(key, 3)
    positions = jnp.arange(NODES).astype(jnp.float32) / (NODES - 1)
    base = jnp.exp(jax.random.uniform(key_base, (NODES, NODES), jnp.float32, math.log(0.2), math.log(5.0)))
    row_scale = jnp.exp(jax.random.uniform(key_rows, (NODES, 1), jnp.float32, 0.0, math.log(10.0)))
    col_scale = jnp.exp(jax.random.uniform(key_cols, (1, NODES), jnp.float32, 0.0, math.log(10.0)))
    ramp = 1.0 + 2.0 * positions
    values = base * row_scale * col_scale * ramp[:, None] * float(NODES) ** (-0.5)
    return values.astype(jnp.bfloat16)


def draw_tile_pattern(key, part):
    key_level, key_force, key_order = jax.random.split(key, 3)
    block_rows = NT // RT
    block_cols = NT // KT
    levels = jax.random.randint(key_level, (block_rows, block_cols), 0, 4).astype(jnp.int32)
    forced = jax.random.randint(key_force, (), 0, block_rows * block_cols).astype(jnp.int32)
    block_ids = jnp.arange(block_rows * block_cols).astype(jnp.int32).reshape(block_rows, block_cols)
    levels = jnp.where(block_ids == forced, 0, levels)
    targets = jnp.right_shift(jnp.full((block_rows, block_cols), KDEV, jnp.int32), levels)
    row_ids = jnp.arange(NT).astype(jnp.int32)[:, None]
    col_ids = jnp.arange(NT).astype(jnp.int32)[None, :]
    diagonal = (row_ids == col_ids).astype(jnp.int32)
    scores = jax.random.permutation(key_order, NT * NT).astype(jnp.int32).reshape(NT, NT) + diagonal * (NT * NT)
    grouped = scores.reshape(block_rows, RT, block_cols, KT).transpose(0, 2, 1, 3).reshape(block_rows, block_cols, RT * KT)
    diag_grouped = diagonal.reshape(block_rows, RT, block_cols, KT).transpose(0, 2, 1, 3).reshape(block_rows, block_cols, RT * KT)
    ranks = jnp.sum((grouped[..., None, :] > grouped[..., :, None]).astype(jnp.int32), axis=-1)
    needed = jnp.maximum(jnp.maximum(targets, jnp.sum(diag_grouped, axis=-1)), 1)
    chosen = (ranks < needed[..., None]).astype(jnp.int32)
    return chosen.reshape(block_rows, block_cols, RT, KT).transpose(0, 2, 1, 3).reshape(NT, NT)


def draw_kept_tiles(key, part):
    panel_tiles = PT * N_COL
    kept = (jax.random.randint(key, (NT, panel_tiles), 0, 4) > 0).astype(jnp.int32)
    col_ids = jnp.arange(panel_tiles).astype(jnp.int32)
    home_rows = col_ids // PT * KT + col_ids % PT
    row_ids = jnp.arange(NT).astype(jnp.int32)[:, None]
    return jnp.where(row_ids == home_rows[None, :], 1, kept).astype(jnp.int32)


def setup_inputs(seed: int = 0) -> dict:
    splits = jax.random.split(jax.random.key(seed), 4)
    return {
        "transition": draw_transition(jax.random.fold_in(splits[3], 71), 0),
        "tile_pattern": draw_tile_pattern(jax.random.fold_in(splits[3], 71), 0),
        "kept_tiles": draw_kept_tiles(jax.random.fold_in(splits[3], 71), 0),
    }


def expand_tiles(tile_mask):
    return jnp.repeat(jnp.repeat(tile_mask, TILE, axis=0), TILE, axis=1)


def reference(transition, tile_pattern, kept_tiles):
    masked = transition * expand_tiles(tile_pattern).astype(jnp.bfloat16)
    column_panel = masked.reshape(NODES, N_COL, KT * TILE)[:, :, :PT * TILE].reshape(NODES, PANEL)
    product = jnp.dot(masked, column_panel, preferred_element_type=jnp.float32)
    pruned = product * expand_tiles(kept_tiles).astype(jnp.float32)
    inflated = pruned * pruned
    col_sums = jnp.sum(inflated, axis=0)
    squares = jnp.sum(inflated * inflated, axis=0)
    normalized = inflated / col_sums
    spread = squares / (col_sums * col_sums)
    chaos_value = jnp.max(jnp.max(normalized, axis=0) - spread)
    return normalized * NODES, chaos_value * NODES
```

```python
import jax
import jax.numpy as jnp
from jax import lax
from jax.experimental import pallas as pl
from jax.experimental.pallas import tpu as pltpu
from jax.sharding import PartitionSpec as P


def split_axis(size):
    minor = 1
    while minor * minor * 4 <= size:
        minor *= 2
    return size // minor, minor


def pack_tiles(transition, tile_pattern, width, cap):
    rows, cols = transition.shape
    row_tiles, col_tiles = tile_pattern.shape
    t = rows // row_tiles

    def kernel(pat_ref, x_ref, out_ref, panel_ref):
        n = jnp.int32(0)
        for i in range(row_tiles):
            for k in range(col_tiles):
                on = pat_ref[i, k] > 0

                @pl.when(on & (n < cap))
                def _(i=i, k=k, n=n):
                    out_ref[pl.ds(pl.multiple_of(n * t, t), t), :] = x_ref[i * t:(i + 1) * t, k * t:(k + 1) * t]

                if (k + 1) * t <= width:
                    tile = x_ref[i * t:(i + 1) * t, k * t:(k + 1) * t]
                    panel_ref[i * t:(i + 1) * t, k * t:(k + 1) * t] = jnp.where(on, tile, jnp.zeros_like(tile))
                n = n + on.astype(jnp.int32)

    return pl.pallas_call(
        kernel,
        out_shape=(
            jax.ShapeDtypeStruct((cap * t, t), transition.dtype),
            jax.ShapeDtypeStruct((rows, width), transition.dtype),
        ),
        in_specs=[pl.BlockSpec(memory_space=pltpu.SMEM), pl.BlockSpec(memory_space=pltpu.VMEM)],
        out_specs=(pl.BlockSpec(memory_space=pltpu.VMEM), pl.BlockSpec(memory_space=pltpu.VMEM)),
        cost_estimate=pl.CostEstimate(flops=0, bytes_accessed=2 * rows * cols * 2, transcendentals=0),
        name="pack",
    )(tile_pattern, transition)


def make_expand(row_tiles, col_tiles, t, width, cap, chunk):
    slab = col_tiles * t

    def expand(blocks, meta, patterns, panels, acc=None, kept=None):
        nb = len(blocks)
        steps = row_tiles // chunk
        has_acc = acc is not None

        def kernel(meta_ref, pat_ref, kept_ref, *refs):
            buf_refs = refs[:nb]
            panel_refs = refs[nb:2 * nb]
            pos = 2 * nb
            acc_ref = refs[pos] if has_acc else None
            pos += has_acc
            out_ref = refs[pos]
            pos += 1
            if kept is not None:
                stat_ref = refs[pos]
                pos += 1
            strip_ref, count_ref = refs[pos], refs[pos + 1]
            g = pl.program_id(0)

            @pl.when(g == 0)
            def _():
                for b in range(nb):
                    count_ref[b] = 0

            if has_acc:
                out_ref[...] = acc_ref[...]
            else:
                out_ref[...] = jnp.zeros_like(out_ref)
            for b in range(nb):
                @pl.when(meta_ref[b, 1] > 0)
                def _(b=b):
                    base = meta_ref[b, 0]
                    n = count_ref[b]
                    for i in range(chunk):
                        for k in range(col_tiles):
                            on = pat_ref[base, (g * chunk + i) * col_tiles + k] > 0
                            at = pl.multiple_of(jnp.minimum(n, cap - 1) * t, t)
                            tile = buf_refs[b][pl.ds(at, t), :]
                            strip_ref[i * t:(i + 1) * t, k * t:(k + 1) * t] = jnp.where(on, tile, jnp.zeros_like(tile))
                            n = n + on.astype(jnp.int32)
                    count_ref[b] = n
                    out_ref[...] += jnp.dot(strip_ref[...], panel_refs[b][...], preferred_element_type=jnp.float32)

            if kept is not None:
                sums, squares, peaks = [], [], []
                for j in range(width // t):
                    total = jnp.zeros((8, t), jnp.float32)
                    square = jnp.zeros((8, t), jnp.float32)
                    peak = jnp.zeros((8, t), jnp.float32)
                    for i in range(chunk):
                        keep = kept_ref[g * chunk + i, j].astype(jnp.float32)
                        pruned = out_ref[i * t:(i + 1) * t, j * t:(j + 1) * t] * keep
                        inflated = pruned * pruned
                        out_ref[i * t:(i + 1) * t, j * t:(j + 1) * t] = inflated
                        grouped = inflated.reshape(t // 8, 8, t)
                        total += jnp.sum(grouped, axis=0)
                        square += jnp.sum(grouped * grouped, axis=0)
                        peak = jnp.maximum(peak, jnp.max(grouped, axis=0))
                    sums.append(total)
                    squares.append(square)
                    peaks.append(peak)
                total = jnp.sum(jnp.concatenate(sums, axis=1), axis=0, keepdims=True)
                square = jnp.sum(jnp.concatenate(squares, axis=1), axis=0, keepdims=True)
                peak = jnp.max(jnp.concatenate(peaks, axis=1), axis=0, keepdims=True)

                @pl.when(g == 0)
                def _():
                    stat_ref[0:1, :] = total
                    stat_ref[1:2, :] = square
                    stat_ref[2:3, :] = peak

                @pl.when(g > 0)
                def _():
                    stat_ref[0:1, :] += total
                    stat_ref[1:2, :] += square
                    stat_ref[2:3, :] = jnp.maximum(stat_ref[2:3, :], peak)

        acc_spec = pl.BlockSpec((chunk * t, width), lambda g, m, p, k: (g, 0))
        in_specs = [pl.BlockSpec((cap * t, t), lambda g, m, p, k: (0, 0))] * nb
        in_specs += [
            pl.BlockSpec((pl.Squeezed(), slab, width), lambda g, m, p, k, b=b: (m[b, 2], 0, 0)) for b in range(nb)
        ]
        out_shape = [jax.ShapeDtypeStruct((row_tiles * t, width), jnp.float32)]
        out_specs = [acc_spec]
        args = [*blocks, *[panels] * nb]
        if has_acc:
            in_specs.append(acc_spec)
            args.append(acc)
        if kept is not None:
            out_shape.append(jax.ShapeDtypeStruct((8, width), jnp.float32))
            out_specs.append(pl.BlockSpec((8, width), lambda g, m, p, k: (0, 0)))
        out = pl.pallas_call(
            kernel,
            out_shape=out_shape,
            grid_spec=pltpu.PrefetchScalarGridSpec(
                num_scalar_prefetch=3,
                grid=(steps,),
                in_specs=in_specs,
                out_specs=out_specs,
                scratch_shapes=[pltpu.VMEM((chunk * t, slab), jnp.bfloat16), pltpu.SMEM((nb,), jnp.int32)],
            ),
            input_output_aliases={3 + 2 * nb: 0} if has_acc else {},
            cost_estimate=pl.CostEstimate(
                flops=2 * nb * row_tiles * t * slab * width,
                bytes_accessed=nb * (cap * t * t + slab * width) * 2 + 2 * row_tiles * t * width * 4,
                transcendentals=0,
            ),
            name="expand",
        )(meta, patterns, kept if kept is not None else jnp.zeros((row_tiles, width // t), jnp.int32), *args)
        return out if kept is not None else out[0]

    return expand


def body(transition, tile_pattern, kept_tiles):
    row_tiles, col_tiles = tile_pattern.shape
    t = transition.shape[0] // row_tiles
    width = kept_tiles.shape[1] * t
    cap = row_tiles * col_tiles // 2
    n_row, n_col = lax.axis_size("row"), lax.axis_size("col")
    major, minor = split_axis(n_col)
    n_y = n_row // 2
    ratio = row_tiles // col_tiles
    r, c = lax.axis_index("row"), lax.axis_index("col")
    z, x = c // minor, c % minor

    def along_z(a, step, direction):
        pairs = []
        for i in range(major):
            src, dst = i, i + direction
            have = src if direction > 0 else major - 1 - src
            if 0 <= dst < major and have >= step - 1:
                pairs += [(src * minor + j, dst * minor + j) for j in range(minor)]
        return lax.ppermute(a, "col", pairs)

    def along_x(a, shift, at):
        return lax.ppermute(a, "col", [(i * minor + j, i * minor + (j + shift) % minor) for i in at for j in range(minor)])

    packed, panel = pack_tiles(transition, tile_pattern, width, cap)
    all_z = range(major)

    waves = [[(packed, z, 0)]]
    waves[0] += [(along_x(packed, s, all_z), z, s) for s in range(1, minor)]
    up = down = packed
    for step in range(1, major):
        up, down = along_z(up, step, 1), along_z(down, step, -1)
        waves.append([(up, z - step, 0), (down, z + step, 0)])
        waves.append([
            (along_x(a, s, at), zz, s)
            for a, zz, at in ((up, z - step, range(step, major)), (down, z + step, range(0, major - step)))
            for s in range(1, minor)
        ])

    pieces = []
    for s in range(n_y):
        there = panel if s == 0 else lax.ppermute(
            panel, "row", [(i * 2 + k, (i + s) % n_y * 2 + k) for i in range(n_y) for k in range(2)])
        other = lax.ppermute(there, "row", [(i, i ^ 1) for i in range(n_row)])
        pieces += [there, other]
    panels = jnp.concatenate(pieces, axis=0).reshape(n_row * ratio, col_tiles * t, width)

    patterns = lax.all_gather(tile_pattern.reshape(-1), "col", axis=0)
    expand = make_expand(row_tiles, col_tiles, t, width, cap, 4)

    def describe(zz, shift):
        valid = (zz >= 0) & (zz < major)
        col = jnp.clip(zz, 0, major - 1) * minor + (x - shift) % minor
        owner, half = col // ratio, col % ratio
        place = ((r // 2 - owner // 2) % n_y * 2 + ((r ^ owner) & 1)) * ratio + half
        return jnp.stack([col, valid.astype(jnp.int32), place])

    acc = None
    for w, wave in enumerate(waves):
        meta = jnp.stack([describe(zz, s) for _, zz, s in wave]).astype(jnp.int32)
        last = w == len(waves) - 1
        acc = expand([a for a, _, _ in wave], meta, patterns, panels, acc, kept_tiles if last else None)
    inflated, stats = acc

    col_sums, squares = lax.psum((stats[0], stats[1]), "row")
    col_peaks = lax.pmax(stats[2], "row")
    normalized = inflated / col_sums
    spread = squares / (col_sums * col_sums)
    node_count = transition.shape[0] * n_row
    local_max = jnp.max(col_peaks / col_sums - spread)
    chaos_value = lax.pmax(local_max, "col")
    return normalized * node_count, chaos_value * node_count


def solution(mesh):
    placed = (P("row", "col"), P("row", "col"), P("row", "col"))
    return jax.shard_map(
        body, mesh=mesh, in_specs=placed, out_specs=(P("row", "col"), P()), check_vma=False
    )
```

```python
import numpy as np
import jax
import jax.numpy as jnp
from jax import lax
from jax.experimental import pallas as pl
from jax.experimental.pallas import tpu as pltpu
from jax.sharding import PartitionSpec as P


NOTE = 16


def split_axis(size):
    minor = 1
    while minor * minor * 4 <= size:
        minor *= 2
    return size // minor, minor


def pack_tiles(transition, tile_pattern, width):
    rows, cols = transition.shape
    row_tiles, col_tiles = tile_pattern.shape
    t = rows // row_tiles
    half = row_tiles * col_tiles // 4
    half_rows = half * t + NOTE

    def kernel(pat_ref, x_ref, out_ref, panel_ref):
        n = jnp.int32(0)
        lane = lax.broadcasted_iota(jnp.int32, (NOTE, t), 1)
        note = jnp.zeros((NOTE, t), jnp.float32)
        for i in range(row_tiles):
            for k in range(col_tiles):
                on = pat_ref[i, k] > 0
                at = pl.multiple_of(n * t + jnp.where(n >= half, NOTE, 0), NOTE)

                @pl.when(on & (n < 2 * half))
                def _(i=i, k=k, at=at):
                    out_ref[pl.ds(at, t), :] = x_ref[i * t:(i + 1) * t, k * t:(k + 1) * t]

                if (k + 1) * t <= width:
                    tile = x_ref[i * t:(i + 1) * t, k * t:(k + 1) * t]
                    panel_ref[i * t:(i + 1) * t, k * t:(k + 1) * t] = jnp.where(on, tile, jnp.zeros_like(tile))
                note = jnp.where(lane == i * col_tiles + k, on.astype(jnp.float32), note)
                n = n + on.astype(jnp.int32)
        for h in range(2):
            out_ref[h * half_rows + half * t:(h + 1) * half_rows, :] = note.astype(out_ref.dtype)

    return pl.pallas_call(
        kernel,
        out_shape=(
            jax.ShapeDtypeStruct((2 * half_rows, t), transition.dtype),
            jax.ShapeDtypeStruct((rows, width), transition.dtype),
        ),
        in_specs=[pl.BlockSpec(memory_space=pltpu.SMEM), pl.BlockSpec(memory_space=pltpu.VMEM)],
        out_specs=(pl.BlockSpec(memory_space=pltpu.VMEM), pl.BlockSpec(memory_space=pltpu.VMEM)),
        cost_estimate=pl.CostEstimate(flops=0, bytes_accessed=2 * rows * cols * 2, transcendentals=0),
        name="pack",
    )(tile_pattern, transition)


def expand(blocks, meta, first, panels, acc, kept, row_tiles, chunk):
    nb = len(blocks)
    _, slab, width = panels.shape
    t = blocks[0][0].shape[1]
    col_tiles = slab // t
    half = row_tiles * col_tiles // 4
    half_rows = half * t + NOTE
    has_acc = acc is not None
    arrays, notes, where = [], [], []
    for block in blocks:
        where.append(len(arrays))
        arrays += block
        notes.append(block[0][half * t:half * t + 8].astype(jnp.int32))
    n_pre = 2 + nb

    def kernel(*refs):
        meta_ref, kept_ref = refs[:2]
        pat_refs = refs[2:n_pre]
        pos = n_pre
        buf_refs = refs[pos:pos + len(arrays)]
        pos += len(arrays)
        panel_refs = refs[pos:pos + nb]
        pos += nb
        acc_ref = refs[pos] if has_acc else None
        pos += has_acc
        out_ref = refs[pos]
        pos += 1
        if kept is not None:
            stat_ref = refs[pos]
            pos += 1
        strip_ref, count_ref = refs[pos], refs[pos + 1]
        g = pl.program_id(0)

        @pl.when(g == 0)
        def _():
            for b in range(nb):
                count_ref[b] = 0

        out_ref[...] = acc_ref[...] if has_acc else jnp.zeros_like(out_ref)
        for b in range(nb):
            @pl.when(meta_ref[first + b, 0] > 0)
            def _(b=b):
                n = count_ref[b]
                for i in range(chunk):
                    for k in range(col_tiles):
                        on = pat_refs[b][0, (g * chunk + i) * col_tiles + k] > 0
                        slot = jnp.minimum(n, 2 * half - 1)
                        if len(blocks[b]) == 1:
                            at = pl.multiple_of(slot * t + jnp.where(slot >= half, NOTE, 0), NOTE)
                            tile = buf_refs[where[b]][pl.ds(at, t), :]
                        else:
                            at = pl.multiple_of(jnp.where(slot >= half, slot - half, slot) * t, NOTE)
                            tile = jnp.where(
                                slot >= half, buf_refs[where[b] + 1][pl.ds(at, t), :], buf_refs[where[b]][pl.ds(at, t), :])
                        strip_ref[i * t:(i + 1) * t, k * t:(k + 1) * t] = jnp.where(on, tile, jnp.zeros_like(tile))
                        n = n + on.astype(jnp.int32)
                count_ref[b] = n
                out_ref[...] += jnp.dot(strip_ref[...], panel_refs[b][...], preferred_element_type=jnp.float32)

        if kept is not None:
            sums, squares, peaks = [], [], []
            for j in range(width // t):
                total = jnp.zeros((8, t), jnp.float32)
                square = jnp.zeros((8, t), jnp.float32)
                peak = jnp.zeros((8, t), jnp.float32)
                for i in range(chunk):
                    keep = kept_ref[g * chunk + i, j].astype(jnp.float32)
                    pruned = out_ref[i * t:(i + 1) * t, j * t:(j + 1) * t] * keep
                    inflated = pruned * pruned
                    out_ref[i * t:(i + 1) * t, j * t:(j + 1) * t] = inflated
                    grouped = inflated.reshape(t // 8, 8, t)
                    total += jnp.sum(grouped, axis=0)
                    square += jnp.sum(grouped * grouped, axis=0)
                    peak = jnp.maximum(peak, jnp.max(grouped, axis=0))
                sums.append(total)
                squares.append(square)
                peaks.append(peak)
            total = jnp.sum(jnp.concatenate(sums, axis=1), axis=0, keepdims=True)
            square = jnp.sum(jnp.concatenate(squares, axis=1), axis=0, keepdims=True)
            peak = jnp.max(jnp.concatenate(peaks, axis=1), axis=0, keepdims=True)

            @pl.when(g == 0)
            def _():
                stat_ref[0:1, :] = total
                stat_ref[1:2, :] = square
                stat_ref[2:3, :] = peak

            @pl.when(g > 0)
            def _():
                stat_ref[0:1, :] += total
                stat_ref[1:2, :] += square
                stat_ref[2:3, :] = jnp.maximum(stat_ref[2:3, :], peak)

    acc_spec = pl.BlockSpec((chunk * t, width), lambda g, *p: (g, 0))
    in_specs = [pl.BlockSpec(a.shape, lambda g, *p: (0, 0)) for a in arrays]
    in_specs += [
        pl.BlockSpec((pl.Squeezed(), slab, width), lambda g, m, *p, b=b: (m[first + b, 1], 0, 0)) for b in range(nb)
    ]
    out_shape = [jax.ShapeDtypeStruct((row_tiles * t, width), jnp.float32)]
    out_specs = [acc_spec]
    args = [*arrays, *[panels] * nb]
    if has_acc:
        in_specs.append(acc_spec)
        args.append(acc)
    if kept is not None:
        out_shape.append(jax.ShapeDtypeStruct((8, width), jnp.float32))
        out_specs.append(pl.BlockSpec((8, width), lambda g, *p: (0, 0)))
    out = pl.pallas_call(
        kernel,
        out_shape=out_shape,
        grid_spec=pltpu.PrefetchScalarGridSpec(
            num_scalar_prefetch=n_pre,
            grid=(row_tiles // chunk,),
            in_specs=in_specs,
            out_specs=out_specs,
            scratch_shapes=[pltpu.VMEM((chunk * t, slab), jnp.bfloat16), pltpu.SMEM((nb,), jnp.int32)],
        ),
        input_output_aliases={n_pre + len(arrays) + nb: 0} if has_acc else {},
        cost_estimate=pl.CostEstimate(
            flops=2 * nb * row_tiles * t * slab * width,
            bytes_accessed=nb * (2 * half_rows * t + slab * width) * 2 + 2 * row_tiles * t * width * 4,
            transcendentals=0,
        ),
        name="expand",
    )(meta, kept if kept is not None else meta, *notes, *args)
    return out if kept is not None else out[0]


def gather_general(packed, major, minor):
    def line(a, step, direction):
        pairs = []
        for i in range(major):
            have = i if direction > 0 else major - 1 - i
            if 0 <= i + direction < major and have >= step - 1:
                pairs += [(i * minor + j, (i + direction) * minor + j) for j in range(minor)]
        return lax.ppermute(a, "col", pairs)

    def turn(a, shift, at):
        return lax.ppermute(a, "col", [(i * minor + j, i * minor + (j + shift) % minor) for i in at for j in range(minor)])

    here = list(range(major))
    waves = [[([packed], here, 0)] + [([turn(packed, s, here)], here, s) for s in range(1, minor)]]
    up = down = packed
    for step in range(1, major):
        up, down = line(up, step, 1), line(down, step, -1)
        below = [i - step if i >= step else -1 for i in here]
        above = [i + step if i + step < major else -1 for i in here]
        waves.append([([up], below, 0), ([down], above, 0)])
        waves.append([
            ([turn(a, s, [i for i in here if at[i] >= 0])], at, s) for a, at in ((up, below), (down, above)) for s in range(1, minor)
        ])
    return waves


def gather_4x2(packed):
    rows = packed.shape[0] // 2

    def z(a, pairs):
        return lax.ppermute(a, "col", [(i * 2 + j, k * 2 + j) for i, k in pairs for j in range(2)])

    def x(a, at):
        return lax.ppermute(a, "col", [(i * 2 + j, i * 2 + 1 - j) for i in at for j in range(2)])

    d1 = z(packed, [(1, 0), (2, 1), (3, 2)])
    u1 = z(packed, [(0, 1), (1, 2), (2, 3)])
    x0 = x(packed, range(4))
    d2 = z(d1, [(1, 0), (2, 1)])
    u2 = z(u1, [(1, 2), (2, 3)])
    xd1 = x(d1, (0, 1))
    xu1 = x(u1, (2, 3))
    e = z(x0, [(0, 1), (3, 2)])
    d3 = z(d2, [(1, 0)])
    u3 = z(u2, [(2, 3)])
    xd2a = x(d2[:rows], (0, 1))
    xu2a = x(u2[:rows], (2, 3))
    xd2b = x(d2[rows:], (0, 1))
    xu2b = x(u2[rows:], (2, 3))
    fd = z(xd2a, [(1, 0)])
    fu = z(xu2a, [(2, 3)])
    xd3b = x(d3[rows:], (0,))
    xu3b = x(u3[rows:], (3,))
    return [
        [([packed], [0, 1, 2, 3], 0), ([x0], [0, 1, 2, 3], 1)],
        [([d1], [1, 2, 3, -1], 0), ([u1], [-1, 0, 1, 2], 0)],
        [([d2], [2, 3, -1, -1], 0), ([u2], [-1, -1, 0, 1], 0)],
        [([xd1], [1, 2, -1, -1], 1), ([xu1], [-1, -1, 1, 2], 1), ([e], [-1, 0, 3, -1], 1)],
        [
            ([d3], [3, -1, -1, -1], 0), ([u3], [-1, -1, -1, 0], 0),
            ([xd2a, xd2b], [2, 3, -1, -1], 1), ([xu2a, xu2b], [-1, -1, 0, 1], 1),
        ],
        [([fd, xd3b], [3, -1, -1, -1], 1), ([fu, xu3b], [-1, -1, -1, 0], 1)],
    ]


def body(transition, tile_pattern, kept_tiles):
    row_tiles, col_tiles = tile_pattern.shape
    t = transition.shape[0] // row_tiles
    width = kept_tiles.shape[1] * t
    n_row, n_col = lax.axis_size("row"), lax.axis_size("col")
    major, minor = split_axis(n_col)
    n_y = n_row // 2
    ratio = row_tiles // col_tiles
    r, c = lax.axis_index("row"), lax.axis_index("col")

    packed, panel = pack_tiles(transition, tile_pattern, width)
    waves = gather_4x2(packed) if (major, minor) == (4, 2) else gather_general(packed, major, minor)

    pieces = []
    for s in range(n_y):
        there = panel if s == 0 else lax.ppermute(
            panel, "row", [(i * 2 + k, (i + s) % n_y * 2 + k) for i in range(n_y) for k in range(2)])
        pieces += [there, lax.ppermute(there, "row", [(i, i ^ 1) for i in range(n_row)])]
    panels = jnp.concatenate(pieces, axis=0).reshape(n_row * ratio, col_tiles * t, width)

    flat = [entry for wave in waves for entry in wave]
    source = jnp.asarray(np.array([at for _, at, _ in flat], np.int32).T)[c // minor]
    col = jnp.maximum(source, 0) * minor + (c % minor - jnp.asarray(np.array([s for _, _, s in flat], np.int32))) % minor
    owner = col // ratio
    place = ((r // 2 - owner // 2) % n_y * 2 + (r + owner) % 2) * ratio + col % ratio
    meta = jnp.stack([(source >= 0).astype(jnp.int32), place], axis=1).astype(jnp.int32)

    acc, first = None, 0
    for w, wave in enumerate(waves):
        last = w == len(waves) - 1
        acc = expand([a for a, _, _ in wave], meta, first, panels, acc, kept_tiles if last else None, row_tiles, 4)
        first += len(wave)
    inflated, stats = acc

    col_sums, squares = lax.psum((stats[0], stats[1]), "row")
    col_peaks = lax.pmax(stats[2], "row")
    normalized = inflated / col_sums
    spread = squares / (col_sums * col_sums)
    node_count = transition.shape[0] * n_row
    local_max = jnp.max(col_peaks / col_sums - spread)
    chaos_value = lax.pmax(local_max, "col")
    return normalized * node_count, chaos_value * node_count


def solution(mesh):
    placed = (P("row", "col"), P("row", "col"), P("row", "col"))
    return jax.shard_map(body, mesh=mesh, in_specs=placed, out_specs=(P("row", "col"), P()), check_vma=False)
```

```python
import numpy as np
import jax
import jax.numpy as jnp
from jax import lax
from jax.experimental import pallas as pl
from jax.experimental.pallas import tpu as pltpu
from jax.sharding import PartitionSpec as P


NOTE = 16


def split_axis(size):
    minor = 1
    while minor * minor * 4 <= size:
        minor *= 2
    return size // minor, minor


def pack_tiles(transition, pattern_t, width):
    rows, cols = transition.shape
    col_tiles, row_tiles = pattern_t.shape
    t = rows // row_tiles
    cap = row_tiles * col_tiles // 2

    def kernel(pat_ref, x_ref, out_ref, panel_ref):
        n = jnp.int32(0)
        lane = lax.broadcasted_iota(jnp.int32, (NOTE, t), 1)
        note = jnp.zeros((NOTE, t), jnp.float32)
        for i in range(row_tiles):
            for k in range(col_tiles):
                on = pat_ref[k, i] > 0

                @pl.when(on & (n < cap))
                def _(i=i, k=k, n=n):
                    out_ref[pl.ds(pl.multiple_of(n * t, t), t), :] = x_ref[i * t:(i + 1) * t, k * t:(k + 1) * t]

                if (k + 1) * t <= width:
                    tile = x_ref[i * t:(i + 1) * t, k * t:(k + 1) * t]
                    panel_ref[i * t:(i + 1) * t, k * t:(k + 1) * t] = jnp.where(on, tile, jnp.zeros_like(tile))
                note = jnp.where(lane == i * col_tiles + k, on.astype(jnp.float32), note)
                n = n + on.astype(jnp.int32)
        out_ref[cap * t:cap * t + NOTE, :] = note.astype(out_ref.dtype)

    return pl.pallas_call(
        kernel,
        out_shape=(
            jax.ShapeDtypeStruct((cap * t + NOTE, t), transition.dtype),
            jax.ShapeDtypeStruct((rows, width), transition.dtype),
        ),
        in_specs=[pl.BlockSpec(memory_space=pltpu.SMEM), pl.BlockSpec(memory_space=pltpu.VMEM)],
        out_specs=(pl.BlockSpec(memory_space=pltpu.VMEM), pl.BlockSpec(memory_space=pltpu.VMEM)),
        cost_estimate=pl.CostEstimate(flops=0, bytes_accessed=2 * rows * cols * 2, transcendentals=0),
        name="pack",
    )(pattern_t, transition)


def expand(blocks, meta, first, pieces, acc, kept_t, row_tiles, chunk):
    nb, nq = len(blocks), len(pieces)
    _, slab, width = pieces[0].shape
    t = blocks[0].shape[1]
    col_tiles = slab // t
    cap = row_tiles * col_tiles // 2
    has_acc, last = acc is not None, kept_t is not None

    def kernel(*refs):
        refs = list(refs)
        meta_ref = refs.pop(0)
        kept_ref = refs.pop(0) if last else None
        block_refs, refs = refs[:nb], refs[nb:]
        piece_refs, refs = refs[:nq], refs[nq:]
        acc_ref = refs.pop(0) if has_acc else None
        out_ref = refs.pop(0)
        stat_ref = refs.pop(0) if last else None
        buf_ref, slab_ref, note_ref, pat_ref, strip_ref, buf_sem, slab_sem, pat_sem = refs

        def load(b):
            return pltpu.make_async_copy(block_refs[b], buf_ref.at[b], buf_sem.at[b])

        def load_slab(b, q):
            return pltpu.make_async_copy(piece_refs[q].at[meta_ref[first + b, 2]], slab_ref.at[b], slab_sem.at[b])

        for b in range(nb):
            @pl.when(meta_ref[first + b, 0] > 0)
            def _(b=b):
                load(b).start()
                for q in range(nq):
                    @pl.when(meta_ref[first + b, 1] == q)
                    def _(q=q):
                        load_slab(b, q).start()

        if has_acc:
            out_ref[...] = acc_ref[...]
        else:
            out_ref[...] = jnp.zeros_like(out_ref)

        for b in range(nb):
            @pl.when(meta_ref[first + b, 0] > 0)
            def _(b=b):
                load(b).wait()
                note_ref[...] = buf_ref[b, cap * t:cap * t + 8, :].astype(jnp.float32).astype(jnp.int32)
                to_scalar = pltpu.make_async_copy(note_ref, pat_ref, pat_sem)
                to_scalar.start()
                to_scalar.wait()
                load_slab(b, 0).wait()

                def step(g, n):
                    for i in range(chunk):
                        for k in range(col_tiles):
                            on = pat_ref[0, (g * chunk + i) * col_tiles + k] > 0
                            at = pl.multiple_of(jnp.minimum(n, cap - 1) * t, t)
                            tile = buf_ref[b, pl.ds(at, t), :]
                            strip_ref[i * t:(i + 1) * t, k * t:(k + 1) * t] = jnp.where(on, tile, jnp.zeros_like(tile))
                            n = n + on.astype(jnp.int32)
                    rows = pl.ds(pl.multiple_of(g * chunk * t, t), chunk * t)
                    out_ref[rows, :] += jnp.dot(strip_ref[...], slab_ref[b], preferred_element_type=jnp.float32)
                    return n

                lax.fori_loop(0, row_tiles // chunk, step, jnp.int32(0))

        if last:
            stat_ref[...] = jnp.zeros_like(stat_ref)
            for j in range(width // t):
                cols = slice(j * t, (j + 1) * t)

                def tile_row(i, carry, cols=cols, j=j):
                    total, square, peak = carry
                    rows = pl.ds(pl.multiple_of(i * t, t), t)
                    pruned = out_ref[rows, cols] * kept_ref[j, i].astype(jnp.float32)
                    inflated = pruned * pruned
                    out_ref[rows, cols] = inflated
                    grouped = inflated.reshape(t // 8, 8, t)
                    return (
                        total + jnp.sum(grouped, axis=0),
                        square + jnp.sum(grouped * grouped, axis=0),
                        jnp.maximum(peak, jnp.max(grouped, axis=0)),
                    )

                zero = jnp.zeros((8, t), jnp.float32)
                total, square, peak = lax.fori_loop(0, row_tiles, tile_row, (zero, zero, zero))
                stat_ref[0:1, cols] = jnp.sum(total, axis=0, keepdims=True)
                stat_ref[1:2, cols] = jnp.sum(square, axis=0, keepdims=True)
                stat_ref[2:3, cols] = jnp.max(peak, axis=0, keepdims=True)

    smem, vmem, anywhere = (pl.BlockSpec(memory_space=m) for m in (pltpu.SMEM, pltpu.VMEM, pl.ANY))
    args, in_specs = [meta], [smem]
    if last:
        args.append(kept_t)
        in_specs.append(smem)
    args += [*blocks, *pieces]
    in_specs += [anywhere] * (nb + nq)
    out_shape = [jax.ShapeDtypeStruct((row_tiles * t, width), jnp.float32)]
    if has_acc:
        args.append(acc)
        in_specs.append(vmem)
    if last:
        out_shape.append(jax.ShapeDtypeStruct((8, width), jnp.float32))
    out = pl.pallas_call(
        kernel,
        out_shape=out_shape,
        in_specs=in_specs,
        out_specs=[vmem] * len(out_shape),
        scratch_shapes=[
            pltpu.VMEM((nb, cap * t + NOTE, t), jnp.bfloat16),
            pltpu.VMEM((nb, slab, width), jnp.bfloat16),
            pltpu.VMEM((8, t), jnp.int32),
            pltpu.SMEM((8, t), jnp.int32),
            pltpu.VMEM((chunk * t, slab), jnp.bfloat16),
            pltpu.SemaphoreType.DMA((nb,)),
            pltpu.SemaphoreType.DMA((nb,)),
            pltpu.SemaphoreType.DMA,
        ],
        cost_estimate=pl.CostEstimate(
            flops=2 * nb * row_tiles * t * slab * width,
            bytes_accessed=nb * (cap * t * t + slab * width) * 2 + 2 * row_tiles * t * width * 4,
            transcendentals=0,
        ),
        name="expand",
    )(*args)
    return out if last else out[0]


def send(a, axis, pairs):
    return lax.ppermute(a, axis, pairs)


def gather_general(packed, major, minor):
    def line(a, step, direction):
        pairs = []
        for i in range(major):
            have = i if direction > 0 else major - 1 - i
            if 0 <= i + direction < major and have >= step - 1:
                pairs += [(i * minor + j, (i + direction) * minor + j) for j in range(minor)]
        return lax.ppermute(a, "col", pairs)

    def turn(a, shift, at):
        return lax.ppermute(a, "col", [(i * minor + j, i * minor + (j + shift) % minor) for i in at for j in range(minor)])

    here = list(range(major))
    waves = [[(packed, here, 0, -1)] + [(turn(packed, s, here), here, s, -1) for s in range(1, minor)]]
    up = down = packed
    for step in range(1, major):
        up, down = line(up, step, 1), line(down, step, -1)
        below = [i - step if i >= step else -1 for i in here]
        above = [i + step if i + step < major else -1 for i in here]
        waves.append([(up, below, 0, -1), (down, above, 0, -1)])
        waves.append([
            (turn(a, s, [i for i in here if at[i] >= 0]), at, s, -1) for a, at in ((up, below), (down, above)) for s in range(1, minor)
        ])
    return waves


def gather_4x2(packed, n_row):
    def z(a, pairs):
        return send(a, "col", [(i * 2 + j, k * 2 + j) for i, k in pairs for j in range(2)])

    def x(a, at):
        return send(a, "col", [(i * 2 + j, i * 2 + 1 - j) for i in at for j in range(2)])

    def some(a, moves, parity):
        return send(a, ("row", "col"), [(r * 8 + i, r * 8 + k) for r in range(parity, n_row, 2) for i, k in moves])

    outer, inner, inward = [(0, 1), (1, 0), (2, 3), (3, 2)], [(1, 2), (2, 1)], [(1, 0), (2, 3)]
    p = z(packed, outer)
    q = z(packed, inner)
    x0 = x(packed, range(4))
    q2 = z(p, inner)
    p2 = z(q, inward)
    xp = x(p, range(4))
    p3 = z(q2, inward)
    xq2 = x(q2, (1, 2))
    xp2 = x(p2, (0, 3))
    e = z(x0, inner)
    f = some(xq2, [(2 + j, j) for j in range(2)] + [(4 + j, 6 + j) for j in range(2)], 0)
    g = some(p3, [(0, 1), (1, 0), (6, 7), (7, 6)], 1)
    return [
        [(packed, [0, 1, 2, 3], 0, -1), (x0, [0, 1, 2, 3], 1, -1), (p, [1, 0, 3, 2], 0, -1), (q, [-1, 2, 1, -1], 0, -1)],
        [(q2, [-1, 3, 0, -1], 0, -1), (p2, [2, -1, -1, 1], 0, -1), (xp, [1, 0, 3, 2], 1, -1)],
        [
            (p3, [3, -1, -1, 0], 0, -1), (e, [-1, 2, 1, -1], 1, -1),
            (xq2, [-1, 3, 0, -1], 1, -1), (xp2, [2, -1, -1, 1], 1, -1),
        ],
        [(f, [3, -1, -1, 0], 1, 0), (g, [3, -1, -1, 0], 1, 1)],
    ]


def body(transition, tile_pattern, kept_tiles):
    row_tiles, col_tiles = tile_pattern.shape
    t = transition.shape[0] // row_tiles
    width = kept_tiles.shape[1] * t
    n_row, n_col = lax.axis_size("row"), lax.axis_size("col")
    major, minor = split_axis(n_col)
    n_y = n_row // 2
    ratio = row_tiles // col_tiles
    r, c = lax.axis_index("row"), lax.axis_index("col")

    packed, panel = pack_tiles(transition, tile_pattern.T, width)
    waves = gather_4x2(packed, n_row) if (major, minor) == (4, 2) else gather_general(packed, major, minor)

    panel = panel.reshape(ratio, col_tiles * t, width)
    pieces = []
    for s in range(n_y):
        there = panel if s == 0 else send(
            panel, "row", [(i * 2 + k, (i + s) % n_y * 2 + k) for i in range(n_y) for k in range(2)])
        pieces += [there, send(there, "row", [(i, i ^ 1) for i in range(n_row)])]

    flat = [entry for wave in waves for entry in wave]
    source = jnp.asarray(np.array([at for _, at, _, _ in flat], np.int32).T)[c // minor]
    parity = jnp.asarray(np.array([only for _, _, _, only in flat], np.int32))
    col = jnp.maximum(source, 0) * minor + (c + minor - jnp.asarray(np.array([s for _, _, s, _ in flat], np.int32))) % minor
    owner = col // ratio
    here = (source >= 0) & ((parity < 0) | (parity == r % 2))
    piece = (r // 2 + n_y - owner // 2) % n_y * 2 + (r + owner) % 2
    meta = jnp.stack([here.astype(jnp.int32), piece, col % ratio], axis=1).astype(jnp.int32)

    acc, first = None, 0
    for w, wave in enumerate(waves):
        last = w == len(waves) - 1
        acc = expand([a for a, _, _, _ in wave], meta, first, pieces, acc, kept_tiles.T if last else None, row_tiles, 4)
        first += len(wave)
    inflated, stats = acc

    bit = 1
    while bit < n_row:
        other = lax.ppermute(stats, "row", [(i, i ^ bit) for i in range(n_row)])
        added = lax.broadcasted_iota(jnp.int32, stats.shape, 0) < 2
        stats = jnp.where(added, stats + other, jnp.maximum(stats, other))
        bit *= 2
    col_sums, squares, col_peaks = stats[0], stats[1], stats[2]
    normalized = inflated / col_sums
    spread = squares / (col_sums * col_sums)
    node_count = transition.shape[0] * n_row
    chaos_value = jnp.full((8, 128), jnp.max(col_peaks / col_sums - spread))
    bit = 1
    while bit < n_col:
        chaos_value = jnp.maximum(chaos_value, lax.ppermute(chaos_value, "col", [(i, i ^ bit) for i in range(n_col)]))
        bit *= 2
    return normalized * node_count, chaos_value[0, 0] * node_count


def solution(mesh):
    placed = (P("row", "col"), P("row", "col"), P("row", "col"))
    step = jax.shard_map(body, mesh=mesh, in_specs=placed, out_specs=(P("row", "col"), P()), check_vma=False)
    if split_axis(mesh.shape["col"]) != (4, 2):
        return step
    return step
```
